32 devices in a mesh: dp: 4 (over x, core), tensor: 8 (over z, y).
Axes of the slice: x: 2, y: 2, z: 4, core: 2. Of those that a mesh axis runs over, the one named last changes fastest.
Arguments:
- hidden: bfloat16 [3072, 4096], P('dp', 'tensor'), may hold values from -2000 to 2000
- out_embed: bfloat16 [16384, 4096], P('tensor', 'dp'), may hold values from -0.3 to 0.3
- labels: int32 [3072], P('dp'), may hold values from 0 to 16383
Outputs:
- token_loss: float32 [3072], P(('dp', 'tensor'))
- mean_loss: float32 [], replicated
The draws below stay inside these ranges and needn't reach their ends.
All inputs are finite; a program needn't handle non-finite values.
Results may differ from the reference program's by a relative error of at most 0.0003.
Values may be sent and summed in bfloat16 or wider, within the bound.
No kernel may reach another device: no remote copies, remote signals or barrier semaphores. Data moves between devices by JAX's collectives and lax.ppermute only.
A program may use at most 128 MiB of HBM per device.

```python
import math
import jax
import jax.numpy as jnp
import numpy as np
from jax import lax

D = 4096
VOCAB = 16384
TOKENS = 3072


def embed_values(key):
    embed_key = jax.random.fold_in(key, 7)
    values = jnp.clip(jax.random.normal(embed_key, (VOCAB, D), jnp.float32) * 0.05, -0.3, 0.3)
    return values.astype(jnp.bfloat16).astype(jnp.float32)


def draw_out_embed(key, part):
    return embed_values(key).astype(jnp.bfloat16)


def draw_hidden(key, part):
    noise_key = jax.random.fold_in(jax.random.fold_in(key, 11), 0)
    pick_key = jax.random.fold_in(jax.random.fold_in(key, 11), 2)
    first_key = jax.random.fold_in(jax.random.fold_in(key, 11), 3)
    second_key = jax.random.fold_in(jax.random.fold_in(key, 11), 4)
    power_key = jax.random.fold_in(jax.random.fold_in(key, 11), 5)
    gap_key = jax.random.fold_in(jax.random.fold_in(key, 11), 6)
    values = jnp.clip(jax.random.normal(noise_key, (TOKENS, D), jnp.float32), -6.0, 6.0)
    embed = embed_values(key)
    chosen = jax.random.randint(pick_key, (TOKENS,), 0, 12) == 0
    first_row = jax.random.randint(first_key, (TOKENS,), 0, VOCAB)
    second_row = (first_row + 1 + jax.random.randint(second_key, (TOKENS,), 0, VOCAB - 1)) % VOCAB
    strength = jax.random.uniform(power_key, (TOKENS,), jnp.float32, 100.0, 320.0)
    gap = jax.random.uniform(gap_key, (TOKENS,), jnp.float32, 1.0, 3.0)
    first_vec = embed[first_row]
    second_vec = embed[second_row]
    g11 = jnp.sum(first_vec * first_vec, axis=1)
    g22 = jnp.sum(second_vec * second_vec, axis=1)
    g12 = jnp.sum(first_vec * second_vec, axis=1)
    det = g11 * g22 - g12 * g12
    target_one = strength
    target_two = strength - gap
    coef_one = (g22 * target_one - g12 * target_two) / det
    coef_two = (g11 * target_two - g12 * target_one) / det
    aligned = coef_one[:, None] * first_vec + coef_two[:, None] * second_vec
    aligned = jnp.clip(aligned, -2000.0, 2000.0)
    values = jnp.where(chosen[:, None], aligned, values)
    return values.astype(jnp.bfloat16)


def set_ends(values, own_key, least, high):
    longest = values.shape.index(max(values.shape))
    spots = []
    for shift in (0, 1):
        where = [jax.random.randint(jax.random.fold_in(own_key, axis), (), 0, length) for axis, length in enumerate(values.shape)]
        where[longest] = (where[longest] + shift) % values.shape[longest]
        spots.append(tuple(where))
    return values.at[spots[0]].set(least).at[spots[1]].set(high)


def cumulative_ranks(count, lean):
    loads = [(1 << 20) // math.isqrt(standing ** lean) + 1 for standing in range(1, count + 1)]
    width = 1 + sum(loads) // (1 << 30)
    return np.cumsum(np.array([max(1, weight // width) for weight in loads]))


def ranked(key, shape, number_of, skew):
    grid = cumulative_ranks(number_of, skew)
    ticket = jax.random.randint(jax.random.fold_in(key, 1), shape, 0, int(grid[number_of - 1]))
    standing = jnp.searchsorted(jnp.asarray(grid, jnp.int32), ticket, side="right")
    return jax.random.permutation(jax.random.fold_in(key, 2), number_of)[standing].astype(jnp.int32)


def setup_inputs(seed: int = 0) -> dict:
    key_of = jax.random.split(jax.random.key(seed), 4)
    hidden = draw_hidden(jax.random.fold_in(key_of[3], 71), 0)
    out_embed = draw_out_embed(jax.random.fold_in(key_of[3], 71), 0)
    labels = set_ends(ranked(key_of[2], (TOKENS,), VOCAB, 2), jax.random.fold_in(key_of[2], 3), 0, VOCAB - 1).astype(jnp.int32)
    return {"hidden": hidden, "out_embed": out_embed, "labels": labels}


def combine_stats(first, second):
    peak_first, mass_first, label_first = first
    peak_second, mass_second, label_second = second
    peak_value = jnp.maximum(peak_first, peak_second)
    exp_total = mass_first * jnp.exp(peak_first - peak_value) + mass_second * jnp.exp(peak_second - peak_value)
    return (peak_value, exp_total, label_first + label_second)


def reference(hidden, out_embed, labels):
    dense = hidden.astype(jnp.float32)
    row_block = math.gcd(VOCAB, 4096)
    block_total = VOCAB // row_block
    weight_blocks = out_embed.reshape(block_total, row_block, D)
    offsets = (jnp.arange(block_total) * row_block).astype(jnp.int32)

    def absorb(state_now, inputs):
        weight_block, offset = inputs
        logits = jnp.dot(dense, weight_block.astype(jnp.float32).T, precision=lax.Precision.HIGHEST)
        peak_block = jnp.max(logits, axis=1)
        mass_block = jnp.sum(jnp.exp(logits - peak_block[:, None]), axis=1)
        row_ids = offset + lax.broadcasted_iota(jnp.int32, logits.shape, 1)
        label_block = jnp.sum(jnp.where(row_ids == labels[:, None], logits, jnp.zeros_like(logits)), axis=1)
        return combine_stats(state_now, (peak_block, mass_block, label_block)), None

    initial = (jnp.full((TOKENS,), -1e30, jnp.float32), jnp.zeros((TOKENS,), jnp.float32), jnp.zeros((TOKENS,), jnp.float32))
    final_state, unused = lax.scan(absorb, initial, (weight_blocks, offsets))
    peak_value, exp_total, label_logit = final_state
    token_loss = jnp.log(exp_total) + peak_value - label_logit
    return token_loss, jnp.sum(token_loss) / TOKENS
```

```python
import functools

import jax
import jax.numpy as jnp
from jax import lax
from jax.experimental import pallas as pl
from jax.experimental.pallas import tpu as pltpu
from jax.sharding import PartitionSpec as P

CHUNKS = 8


def grid_of(mesh):
    dp, tensor = mesh.shape["dp"], mesh.shape["tensor"]
    y = 1 << ((tensor.bit_length() - 1) // 2)
    return dp // 2, 2, tensor // y, y


class Axis:
    def __init__(self, name, total, size, stride):
        self.name, self.total, self.size, self.stride = name, total, size, stride

    def index(self):
        return lax.rem(lax.div(lax.axis_index(self.name), self.stride), self.size)

    def move(self, value, to):
        pairs = []
        for i in range(self.total):
            p = (i // self.stride) % self.size
            pairs.append((i, i + (to(p) - p) * self.stride))
        return lax.ppermute(value, self.name, pairs)

    def ring(self, value):
        return self.move(value, lambda p: (p + 1) % self.size)

    def swap(self, value, bit):
        return self.move(value, lambda p: p ^ bit)


def chunk_kernel(first, x_offset, shape, place, labels, before, *refs):
    nx, nc, nz, ny = shape
    n_e, n_h = nx * nc, nz * ny
    e_refs, h_refs = refs[:n_e], refs[n_e : n_e + n_h]
    out, e_buf, h_buf, e_sem, h_sem = refs[n_e + n_h :]
    rows, tokens = e_buf.shape[1], h_buf.shape[1]
    x, c, z, y, row0 = (place[i] for i in range(5))
    for i in range(nx):
        for j in range(nc):
            d = lax.rem(x - i + nx, nx) * nc + lax.rem(c - j + nc, nc)
            source = e_refs[i * nc + j]
            if source.shape[0] != rows:
                source = source.at[pl.ds(first, rows)]
            pltpu.make_async_copy(source, e_buf.at[d], e_sem.at[d]).start()
    for s in range(nz):
        for r in range(ny):
            t = lax.rem(z - s + nz, nz) * ny + lax.rem(y - r + ny, ny)
            pltpu.make_async_copy(h_refs[s * ny + r], h_buf.at[t], h_sem.at[t]).start()
    q = n_h // n_e
    width = h_buf.shape[2]
    total = None
    for d in range(n_e):
        pltpu.make_async_copy(e_buf.at[d], e_buf.at[d], e_sem.at[d]).wait()
        for k in range(q):
            t = d * q + k
            pltpu.make_async_copy(h_buf.at[t], h_buf.at[t], h_sem.at[t]).wait()
            part = lax.dot_general(
                e_buf[d, :, k * width : (k + 1) * width],
                h_buf[t],
                (((1,), (1,)), ((), ())),
                preferred_element_type=jnp.float32,
            )
            total = part if total is None else total + part
    peak = jnp.max(total, axis=0, keepdims=True)
    mass = jnp.sum(jnp.exp(total - peak), axis=0, keepdims=True)
    row = row0 + first + lax.broadcasted_iota(jnp.int32, total.shape, 0)
    label = jnp.sum(jnp.where(row == labels[...], total, 0.0), axis=0, keepdims=True)
    old_peak, old_mass, old_label = before[0:1], before[1:2], before[2:3]
    new_peak = jnp.maximum(old_peak, peak)
    out[0:1] = new_peak
    out[1:2] = old_mass * jnp.exp(old_peak - new_peak) + mass * jnp.exp(peak - new_peak)
    out[2:3] = old_label + label


def chunk_stats(first, rows, shape, place, labels, before, e_parts, h_parts):
    n_e, n_h = len(e_parts), len(h_parts)
    tokens, width = h_parts[0].shape
    wide = e_parts[0].shape[1]
    any_space = pl.BlockSpec(memory_space=pl.ANY)
    vmem = pl.BlockSpec(memory_space=pltpu.VMEM)
    return pl.pallas_call(
        functools.partial(chunk_kernel, first, 0, shape),
        out_shape=jax.ShapeDtypeStruct((3, tokens), jnp.float32),
        in_specs=[pl.BlockSpec(memory_space=pltpu.SMEM), vmem, vmem]
        + [any_space] * (n_e + n_h),
        out_specs=vmem,
        scratch_shapes=[
            pltpu.VMEM((n_e, rows, wide), jnp.bfloat16),
            pltpu.VMEM((n_h, tokens, width), jnp.bfloat16),
            pltpu.SemaphoreType.DMA((n_e,)),
            pltpu.SemaphoreType.DMA((n_h,)),
        ],
        compiler_params=pltpu.CompilerParams(vmem_limit_bytes=48 << 20),
        cost_estimate=pl.CostEstimate(
            flops=2 * rows * tokens * width * n_h,
            bytes_accessed=2 * (rows + tokens) * width * n_h,
            transcendentals=rows * tokens,
        ),
        name="chunk_stats",
    )(place, labels, before, *e_parts, *h_parts)


def merge(first, second):
    peak = jnp.maximum(first[0:1], second[0:1])
    mass = first[1:2] * jnp.exp(first[0:1] - peak) + second[1:2] * jnp.exp(second[0:1] - peak)
    return jnp.concatenate([peak, mass, first[2:3] + second[2:3]], axis=0)


def body(shape, hidden, out_embed, labels):
    nx, nc, nz, ny = shape
    x_axis = Axis("dp", nx * nc, nx, nc)
    core = Axis("dp", nx * nc, nc, 1)
    z_axis = Axis("tensor", nz * ny, nz, ny)
    y_axis = Axis("tensor", nz * ny, ny, 1)
    tokens = hidden.shape[0]
    vocab_rows = out_embed.shape[0]
    rows = vocab_rows // CHUNKS
    chunks = [out_embed[k * rows : (k + 1) * rows] for k in range(CHUNKS)]
    arrived = []
    for k in range(CHUNKS):
        mine, parts = chunks[k], [None]
        for _ in range(1, nx):
            mine = x_axis.ring(mine)
            parts.append(mine)
        arrived.append(parts)
    own_swapped = core.ring(out_embed)
    h_parts, held = [], hidden
    for s in range(nz):
        if s:
            held = z_axis.ring(held)
        across = held
        h_parts.append(across)
        for _ in range(1, ny):
            across = y_axis.ring(across)
            h_parts.append(across)
    place = jnp.stack(
        [x_axis.index(), core.index(), z_axis.index(), y_axis.index(), lax.axis_index("tensor") * vocab_rows]
    )
    stats = jnp.concatenate(
        [jnp.full((1, tokens), -jnp.inf, jnp.float32), jnp.zeros((2, tokens), jnp.float32)], axis=0
    )
    label_row = labels.reshape(1, tokens)
    for k in range(CHUNKS):
        e_parts = [out_embed, own_swapped]
        for part in arrived[k][1:]:
            e_parts += [part, core.ring(part)]
        stats = chunk_stats(k * rows, rows, shape, place, label_row, stats, e_parts, h_parts)
    for axis in (y_axis, z_axis):
        bit = 1
        while bit < axis.size:
            stats = merge(stats, axis.swap(stats, bit))
            bit *= 2
    loss = jnp.log(stats[1]) + stats[0] - stats[2]
    share = tokens // lax.axis_size("tensor")
    token_loss = lax.dynamic_slice_in_dim(loss, lax.axis_index("tensor") * share, share)
    total = jnp.broadcast_to(jnp.sum(loss), (8, 128))
    for axis in (core, x_axis):
        bit = 1
        while bit < axis.size:
            total = total + axis.swap(total, bit)
            bit *= 2
    mean_loss = total[0, 0] / (tokens * lax.axis_size("dp"))
    return token_loss, mean_loss


def solution(mesh):
    return jax.shard_map(
        functools.partial(body, grid_of(mesh)),
        mesh=mesh,
        in_specs=(P("dp", "tensor"), P("tensor", "dp"), P("dp")),
        out_specs=(P(("dp", "tensor")), P()),
        check_vma=False,
    )
```
